128 devices in a mesh: wide: 8 (over z_hi, y), narrow: 16 (over x, z_lo, core).
Axes of the slice: x: 4, y: 4, z: 4 (z_hi: 2, z_lo: 2; z = z_hi * 2 + z_lo), core: 2. Of those that a mesh axis runs over, the one named last changes fastest.
Arguments:
- hinv_start: float32 [16384, 16384], P('wide', 'narrow'), as said below
- weights: bfloat16 [2048, 16384], P('narrow', 'wide'), may hold values from -6 to 6
- removed: int32 [1, 512], replicated, may hold values from 0 to 16383, as said below
Outputs:
- hinv_out: float32 [16384, 16384], P('wide', 'narrow')
- weights_out: bfloat16 [2048, 16384], P('narrow', 'wide')
The draws below stay inside these ranges and needn't reach their ends.
Inputs may be any that keep to these rules, and one draw needn't show every extreme that they name: `removed`: all 1 x 512 indices are distinct; 0 and 16383 are always among them. `hinv_start`: symmetric and positive definite.
All inputs are finite; a program needn't handle non-finite values. Where the reference program divides by a largest or mean magnitude, that divisor is 1e-20 or more.
Results may differ from the reference program's by a relative error of at most 0.0036.
Values may be sent and summed in bfloat16 or wider, within the bound.
No kernel may reach another device: no remote copies, remote signals or barrier semaphores. Data moves between devices by JAX's collectives and lax.ppermute only.
A program may use at most 128 MiB of HBM per device.

```python
import jax
import jax.numpy as jnp
from jax import lax

ORDER = 16384
BLK = 512
ROUNDS = 1
ITERS = 8
ROWS = 2048


def draw_removed(key, part):
    inner = jax.random.permutation(jax.random.fold_in(key, 11), ORDER - 2)[:ROUNDS * BLK - 2].astype(jnp.int32) + 1
    ends = jnp.array([0, ORDER - 1], dtype=jnp.int32)
    joined = jnp.concatenate([ends, inner])
    order = jax.random.permutation(jax.random.fold_in(key, 12), ROUNDS * BLK)
    return joined[order].reshape(ROUNDS, BLK).astype(jnp.int32)


def draw_hinv_start(key, part):
    key_diag = jax.random.fold_in(key, 21)
    key_off = jax.random.fold_in(key, 22)
    key_factor = jax.random.fold_in(key, 23)
    rank = ORDER // 8
    diag = jnp.exp(jax.random.uniform(key_diag, (ORDER,), jnp.float32, jnp.log(0.05), jnp.log(20.0)))
    roots = jnp.sqrt(diag)
    raw = jax.random.uniform(key_off, (ORDER, ORDER), jnp.float32, -1.0, 1.0)
    factor = jax.random.normal(key_factor, (ORDER, rank), jnp.float32)
    coeff = 0.125 / jnp.sqrt(ORDER * 2.0 / 3.0)
    shared = jnp.dot(factor, factor.T) / rank
    coupling = (raw + raw.T) * coeff + (shared + shared.T) * 0.5 + jnp.eye(ORDER, dtype=jnp.float32)
    return roots[:, None] * roots[None, :] * coupling


def level_of(rng, shape, shards, smallest, top_value):
    loudness, own = 1.0, jax.random.fold_in(rng, 6)
    for dim, shards_of in shards:
        heights = jnp.exp(jax.random.uniform(jax.random.fold_in(own, dim), (shards_of,), jnp.float32, smallest / len(shards), top_value / len(shards)))
        loudness = loudness * jnp.repeat(heights, shape[dim] // shards_of).reshape([-1 if axis == dim else 1 for axis in range(len(shape))])
    return loudness


def noise(stream_key, dims, scale, limit, pieces=(), kind=jnp.bfloat16):
    result = scale * jax.random.normal(stream_key, dims, jnp.float32)
    if pieces:
        result = result * level_of(stream_key, dims, pieces, -0.22, 0.18)
    return jnp.clip(result, -limit, limit).astype(kind)


def setup_inputs(seed: int = 0) -> dict:
    streams_of = jax.random.split(jax.random.key(seed), 4)
    hinv_start = draw_hinv_start(jax.random.fold_in(streams_of[3], 71), 0)
    weights = noise(streams_of[1], (ROWS, ORDER), 1.0, 6.0, ((0, 16), (1, 8)))
    removed = draw_removed(jax.random.fold_in(streams_of[3], 71), 0)
    return {"hinv_start": hinv_start, "weights": weights, "removed": removed}


def newton_inverse(pivot):
    scale = 1.0 / jnp.max(jnp.sum(jnp.abs(pivot), axis=1))
    identity = jnp.eye(BLK, dtype=jnp.float32)
    approx = identity * scale
    for turn in range(ITERS):
        inner = jnp.dot(pivot, approx, precision=lax.Precision.HIGHEST)
        approx = jnp.dot(approx, 2.0 * identity - inner, precision=lax.Precision.HIGHEST)
    return approx


def reference(hinv_start, weights, removed):
    hess = hinv_start
    wmat = weights
    for step in range(ROUNDS):
        picked = removed[step]
        panel_rows = jnp.take(hess, picked, axis=0)
        panel_cols = jnp.take(hess, picked, axis=1)
        pivot = jnp.take(panel_rows, picked, axis=1)
        inverse = newton_inverse(pivot)
        chosen = jnp.take(wmat, picked, axis=1).astype(jnp.float32)
        gain = jnp.dot(chosen, inverse, precision=lax.Precision.HIGHEST).astype(jnp.bfloat16)
        panel = panel_rows.astype(jnp.bfloat16)
        delta = jnp.dot(gain, panel, preferred_element_type=jnp.float32)
        updated = wmat.astype(jnp.float32) - delta
        updated = updated.at[:, picked].set(0.0)
        wmat = updated.astype(jnp.bfloat16)
        inner = jnp.dot(inverse, panel_rows, precision=lax.Precision.HIGHEST)
        hess = hess - jnp.dot(panel_cols, inner, precision=lax.Precision.HIGHEST)
    return hess, wmat
```

```python
import jax
import jax.numpy as jnp
from jax import lax
from jax.experimental import pallas as pl
from jax.experimental.pallas import tpu as pltpu
from jax.sharding import PartitionSpec as P

ITERS = 8
F32 = jnp.float32
BF16 = jnp.bfloat16
BOTH = ("wide", "narrow")
VMEM = pltpu.MemorySpace.VMEM
SMEM = pltpu.MemorySpace.SMEM


def hop(a, axis, size, move):
    return lax.ppermute(a, axis, [(i, move(i)) for i in range(size)])


def z_hi_swap(a):
    return hop(a, "wide", 8, lambda i: (i + 4) % 8)


def y_step(a, k):
    return hop(a, "wide", 8, lambda i: (i // 4) * 4 + (i + k) % 4)


def core_swap(a):
    return hop(a, "narrow", 16, lambda i: i ^ 1)


def z_lo_swap(a):
    return hop(a, "narrow", 16, lambda i: i ^ 2)


def x_step(a, k):
    return hop(a, "narrow", 16, lambda i: (i + 4 * k) % 16)


def pick_kernel(row_smem, row_vec, col_vec, hess, wmat, pieces, pivot, bands, rows, owned, sem):
    block = rows.shape[0]
    local_rows = hess.shape[0]
    local_cols = hess.shape[1]

    def find(i, count):
        owned[count] = i
        r = row_smem[0, i]
        return count + jnp.where((r >= 0) & (r < local_rows), 1, 0)

    count = lax.fori_loop(0, block, find, 0, unroll=8)

    def band_of(k):
        r = row_smem[0, owned[k]]
        start = pl.multiple_of((r // 8) * 8, 8)
        return r % 8, pltpu.make_async_copy(hess.at[pl.ds(start, 8), :], bands.at[k], sem)

    def fetch(k, carry):
        band_of(k)[1].start()
        return carry

    lax.fori_loop(0, count, fetch, 0)
    rows[...] = jnp.zeros_like(rows)
    ids = lax.broadcasted_iota(jnp.int32, (wmat.shape[1], block), 0)
    hot_w = (ids == row_vec[...]).astype(BF16)
    chosen = jnp.dot(wmat[...], hot_w, preferred_element_type=F32)
    chosen_t = chosen.T.astype(BF16)
    each = block // 8
    for p in range(8):
        pieces[p, block : block + each, :] = chosen_t[p * each : (p + 1) * each, :]
    ids_c = lax.broadcasted_iota(jnp.int32, (local_cols, block), 0)
    hot_c = (ids_c == col_vec[...]).astype(BF16)

    def settle(k, carry):
        band_of(k)[1].wait()
        return carry

    lax.fori_loop(0, count, settle, 0)

    def place(k, carry):
        sub, _ = band_of(k)
        rows[pl.ds(owned[k], 1), :] = bands[k, pl.ds(sub, 1), :]
        return carry

    lax.fori_loop(0, count, place, 0)
    step = 128
    for t in range(block // step):
        part = rows[t * step : (t + 1) * step, :]
        hi = part.astype(BF16)
        rest = part - hi.astype(F32)
        mid = rest.astype(BF16)
        low = (rest - mid.astype(F32)).astype(BF16)
        for p in range(8):
            pieces[p, t * step : (t + 1) * step, :] = hi[:, p * 128 : (p + 1) * 128]
        dot = lambda a: jnp.dot(a, hot_c, preferred_element_type=F32)
        found = (dot(hi) + dot(mid)) + dot(low)
        for g in range(step // 8):
            for c in range(block // 128):
                q = (t * step // 8 + g) * (block // 128) + c
                pivot[q // 2, q % 2] = found[g * 8 : (g + 1) * 8, c * 128 : (c + 1) * 128]


def pick(hess, wmat, row_local, col_local):
    block = row_local.shape[1]
    return pl.pallas_call(
        pick_kernel,
        in_specs=[
            pl.BlockSpec(memory_space=SMEM),
            pl.BlockSpec(memory_space=VMEM),
            pl.BlockSpec(memory_space=VMEM),
            pl.BlockSpec(memory_space=pl.ANY),
            pl.BlockSpec(memory_space=VMEM),
        ],
        out_specs=[pl.BlockSpec(memory_space=VMEM), pl.BlockSpec(memory_space=VMEM)],
        out_shape=[
            jax.ShapeDtypeStruct((8, block + block // 8, 128), BF16),
            jax.ShapeDtypeStruct((128, 2, 8, 128), F32),
        ],
        scratch_shapes=[
            pltpu.VMEM((block, 8, hess.shape[1]), F32),
            pltpu.VMEM((block, hess.shape[1]), F32),
            pltpu.SMEM((block + 1,), jnp.int32),
            pltpu.SemaphoreType.DMA,
        ],
        compiler_params=pltpu.CompilerParams(vmem_limit_bytes=48 * 2**20),
        name="pick",
    )(row_local, row_local, col_local, hess, wmat)


def split(a):
    hi = a.astype(BF16)
    return hi, (a - hi.astype(F32)).astype(BF16)


def update_kernel(tab, inv, rb0, rb1, ru, rd, re, rg, mine, other, cleared, hess, wmat,
                  hess_out, wmat_out, rfull, chosen, t_hi, t_lo, gain):
    t = pl.program_id(0)
    block = inv.shape[0]
    each = block // 8

    @pl.when(t == 0)
    def _():
        slots = [rb0[...], rb1[...], ru[0], ru[1], rd[0], rd[1], re[...], rg[...]]
        for s, slot in enumerate(slots):
            w = tab[s]
            rfull[:, pl.ds(pl.multiple_of(w * 128, 128), 128)] = slot[:block]
            chosen[pl.ds(pl.multiple_of(w * each, each), each), :] = slot[block:]
        x_hi, x_lo = split(inv[...])
        for c in range(0, rfull.shape[1], 256):
            r = rfull[:, c : c + 256]
            part = jnp.dot(x_hi, r, preferred_element_type=F32) + jnp.dot(x_lo, r, preferred_element_type=F32)
            hi, lo = split(part)
            t_hi[:, c : c + 256] = hi
            t_lo[:, c : c + 256] = lo
        ch = chosen[...]
        across = (((0,), (0,)), ((), ()))
        g = lax.dot_general(ch, x_hi, across, preferred_element_type=F32)
        g = g + lax.dot_general(ch, x_lo, across, preferred_element_type=F32)
        gain[...] = g.astype(BF16)

    s0 = tab[16 + 2 * t]
    s1 = tab[17 + 2 * t]

    def work(src):
        left = jnp.concatenate([src[s0], src[s1]], axis=1)
        across = (((0,), (0,)), ((), ()))
        for c in range(0, hess.shape[1], 512):
            d = lax.dot_general(left, t_hi[:, c : c + 512], across, preferred_element_type=F32)
            d = d + lax.dot_general(left, t_lo[:, c : c + 512], across, preferred_element_type=F32)
            hess_out[:, c : c + 512] = hess[:, c : c + 512] - d
        delta = jnp.dot(gain[...], left, preferred_element_type=F32)
        new = wmat[...].astype(F32) - delta
        wmat_out[...] = jnp.where(cleared[...] > 0, 0.0, new).astype(BF16)

    @pl.when(t < 4)
    def _():
        work(mine)

    @pl.when(t >= 4)
    def _():
        work(other)


def update(table, inv, rows, mine, other, cleared, hess, wmat):
    block = inv.shape[0]
    whole = lambda a: pl.BlockSpec(a.shape, lambda t, tab: (0,) * a.ndim)
    grid_spec = pltpu.PrefetchScalarGridSpec(
        num_scalar_prefetch=1,
        grid=(8,),
        in_specs=[whole(inv)] + [whole(r) for r in rows] + [whole(mine), whole(other)] + [
            pl.BlockSpec((1, 256), lambda t, tab: (0, tab[8 + t])),
            pl.BlockSpec((256, hess.shape[1]), lambda t, tab: (tab[8 + t], 0)),
            pl.BlockSpec((wmat.shape[0], 256), lambda t, tab: (0, tab[8 + t])),
        ],
        out_specs=[
            pl.BlockSpec((256, hess.shape[1]), lambda t, tab: (tab[8 + t], 0)),
            pl.BlockSpec((wmat.shape[0], 256), lambda t, tab: (0, tab[8 + t])),
        ],
        scratch_shapes=[
            pltpu.VMEM((block, hess.shape[1]), BF16),
            pltpu.VMEM((block, wmat.shape[0]), BF16),
            pltpu.VMEM((block, hess.shape[1]), BF16),
            pltpu.VMEM((block, hess.shape[1]), BF16),
            pltpu.VMEM((wmat.shape[0], block), BF16),
        ],
    )
    return pl.pallas_call(
        update_kernel,
        grid_spec=grid_spec,
        out_shape=[
            jax.ShapeDtypeStruct(hess.shape, F32),
            jax.ShapeDtypeStruct(wmat.shape, BF16),
        ],
        compiler_params=pltpu.CompilerParams(vmem_limit_bytes=48 * 2**20),
        name="update",
    )(table, inv, *rows, mine, other, cleared, hess, wmat)


def per_device(hinv_start, weights, removed):
    row_count, col_count = hinv_start.shape
    wide = lax.axis_index("wide")
    narrow = lax.axis_index("narrow")
    z_hi, y = wide // 4, wide % 4
    x, z_lo, core = narrow // 4, (narrow // 2) % 2, narrow % 2
    block = removed.shape[1]
    row_start = wide * row_count
    row_local = removed - row_start
    col_local = removed - narrow * col_count
    pieces, pivot_part = pick(hinv_start, weights, row_local, col_local)

    halves = pieces.reshape(2, 4, *pieces.shape[1:])
    keep = lax.dynamic_index_in_dim(halves, z_hi, 0, False)
    send = lax.dynamic_index_in_dim(halves, 1 - z_hi, 0, False)
    kept = keep + z_hi_swap(send)
    quarter = [lax.dynamic_index_in_dim(kept, (y + j) % 4, 0, False) for j in range(4)]
    own = quarter[0] + y_step(quarter[1], 1) + y_step(quarter[3], -1) + y_step(quarter[2], 2)

    parts = lax.all_to_all(pivot_part, BOTH, 0, 0)
    mine_piv = jnp.sum(parts, axis=0)
    spread = jnp.broadcast_to(mine_piv[None], pivot_part.shape)
    tiles = lax.all_to_all(spread, BOTH, 0, 0)
    pivot = tiles.reshape(block // 8, block // 128, 8, 128).transpose(0, 2, 1, 3).reshape(block, block)

    far = z_hi_swap(own)
    near = jnp.stack([own, far])
    up = y_step(near, 1)
    down = y_step(near, -1)
    last_a = y_step(up[0], 1)
    last_b = y_step(down[1], -1)

    swap = [(w * 16 + n, (n // 2) * 16 + 2 * w + n % 2) for w in range(8) for n in range(16)]
    col = lax.ppermute(own[:block], BOTH, swap)
    pair = jnp.stack([col, z_lo_swap(col)])
    cu = x_step(pair, 1)
    cd = x_step(pair, -1)
    ce = x_step(cu[0], 1)
    cg = x_step(cd[1], -1)
    mine = jnp.concatenate([pair, cu, cd, ce[None], cg[None]], axis=0)
    other = core_swap(mine)

    scale = 1.0 / jnp.max(jnp.sum(jnp.abs(pivot), axis=1))
    eye = jnp.eye(block, dtype=F32)
    e = eye - pivot * scale
    p = (eye + e) * scale
    for turn in range(1, ITERS):
        e = jnp.dot(e, e, precision=lax.Precision.HIGH)
        p = p + jnp.dot(p, e, precision=lax.Precision.HIGH)

    i32 = jnp.int32
    w_of = []
    for dy in (0, -1, 1, 2):
        for dz in (0, 1):
            w_of.append(((z_hi + dz) % 2) * 4 + (y + dy) % 4)
    blocks, slots = [], []
    for half in (0, 1):
        for xt in range(4):
            blocks.append((core ^ half) * 4 + xt)
            rel = (xt - x) % 4
            base = jnp.where(rel == 0, 0, jnp.where(rel == 3, 2, jnp.where(rel == 1, 4, 6)))
            for zt in range(2):
                slots.append(base + jnp.where(z_lo == zt, 0, 1))
    table = jnp.stack([v.astype(i32) for v in w_of + blocks + slots])
    ids = row_start + jnp.arange(row_count, dtype=i32)
    cleared = jnp.any(removed[0][:, None] == ids[None, :], axis=0, keepdims=True).astype(F32)
    hess, wmat = update(table, p, [own, far, up, down, last_a, last_b], mine, other, cleared, hinv_start, weights)
    return hess, wmat


def solution(mesh):
    return jax.shard_map(
        per_device,
        mesh=mesh,
        in_specs=(P("wide", "narrow"), P("narrow", "wide"), P()),
        out_specs=(P("wide", "narrow"), P("narrow", "wide")),
        check_vma=False,
    )
```

```python
import functools

import jax
import jax.numpy as jnp
from jax import lax
from jax.experimental import pallas as pl
from jax.experimental.pallas import tpu as pltpu
from jax.sharding import PartitionSpec as P


ITERS = 8
ROOM = 96
F32 = jnp.float32
BF16 = jnp.bfloat16
I32 = jnp.int32
BOTH = ("wide", "narrow")
VMEM = pltpu.MemorySpace.VMEM
SMEM = pltpu.MemorySpace.SMEM


def hop(a, axis, size, move):
    return lax.ppermute(a, axis, [(i, move(i)) for i in range(size)])


def z_hi_swap(a):
    return hop(a, "wide", 8, lambda i: (i + 4) % 8)


def y_step(a, k):
    return hop(a, "wide", 8, lambda i: (i // 4) * 4 + (i + k) % 4)


def core_swap(a):
    return hop(a, "narrow", 16, lambda i: i ^ 1)


def z_lo_swap(a):
    return hop(a, "narrow", 16, lambda i: i ^ 2)


def x_step(a, k):
    return hop(a, "narrow", 16, lambda i: (i + 4 * k) % 16)


def limit(mib):
    return pltpu.CompilerParams(vmem_limit_bytes=mib * 2**20)


def cost(flops, size):
    return pl.CostEstimate(flops=flops, bytes_accessed=size, transcendentals=0)


def split(a):
    hi = a.astype(BF16)
    return hi, (a - hi.astype(F32)).astype(BF16)


def split3(a):
    hi = a.astype(BF16)
    rest = a - hi.astype(F32)
    mid = rest.astype(BF16)
    return hi, mid, (rest - mid.astype(F32)).astype(BF16)


def dot(a, b):
    return jnp.dot(a, b, preferred_element_type=F32)


def exact_dot(a, hot):
    hi, mid, low = split3(a)
    return (dot(hi, hot) + dot(mid, hot)) + dot(low, hot)


def times(left, right):
    (lh, ll), (rh, rl) = left, right
    return dot(lh, rh) + (dot(lh, rl) + dot(ll, rh))


def hot_rows(count, lanes_index):
    ids = lax.broadcasted_iota(I32, (count, lanes_index.shape[1]), 0)
    return (ids == lanes_index).astype(BF16)


def pick_kernel(index_smem, index_vec, hess, wmat, packed, plain, pivot, rows, chosen, wpack, wbuf, owned, sem, wsem):
    block = index_vec.shape[1]
    local_rows, local_cols = hess.shape
    row_start = lax.axis_index("wide") * local_rows
    col_start = lax.axis_index("narrow") * local_cols
    wcopy = pltpu.make_async_copy(wmat, wbuf, wsem)
    wcopy.start()

    def find(i, count):
        owned[count] = i
        r = index_smem[0, i] - row_start
        return count + jnp.where((r >= 0) & (r < local_rows), 1, 0)

    count = jnp.minimum(lax.fori_loop(0, block, find, 0, unroll=16), ROOM)

    def row_of(k):
        return index_smem[0, owned[k]] - row_start

    def row_copy(k):
        return pltpu.make_async_copy(hess.at[pl.ds(row_of(k), 1), :], rows.at[pl.ds(k, 1), :], sem)

    def fetch(k, carry):
        row_copy(k).start()
        return carry

    rows[...] = jnp.zeros_like(rows)
    lax.fori_loop(0, count, fetch, 0)
    wpack[...] = jnp.zeros_like(wpack)
    hot_w = hot_rows(wmat.shape[1], index_vec[...] - row_start)
    wcopy.wait()
    chosen[...] = dot(wbuf[...], hot_w).T
    hot_c = hot_rows(local_cols, index_vec[...] - col_start)

    def settle(k, carry):
        row_copy(k).wait()
        return carry

    def place(k, carry):
        wpack[pl.ds(k, 1), :] = chosen[pl.ds(owned[k], 1), :]
        return carry

    lax.fori_loop(0, count, place, 0)
    lax.fori_loop(0, count, settle, 0)
    found = exact_dot(rows[...], hot_c)
    short = rows[:ROOM, :].astype(BF16)
    packed[:, :local_cols] = short
    plain[...] = short
    packed[:, local_cols:] = wpack[:ROOM, :].astype(BF16)
    turned = found.T
    for d in range(128):
        pivot[d] = turned[d * 4 : (d + 1) * 4, :]


def pick(hess, wmat, removed):
    block = removed.shape[1]
    cols = hess.shape[1]
    return pl.pallas_call(
        pick_kernel,
        in_specs=[
            pl.BlockSpec(memory_space=SMEM),
            pl.BlockSpec(memory_space=VMEM),
            pl.BlockSpec(memory_space=pl.ANY),
            pl.BlockSpec(memory_space=pl.ANY),
        ],
        out_specs=[pl.BlockSpec(memory_space=VMEM)] * 3,
        out_shape=[
            jax.ShapeDtypeStruct((ROOM, cols + 128), BF16),
            jax.ShapeDtypeStruct((ROOM, cols), BF16),
            jax.ShapeDtypeStruct((128, block // 128, 128), F32),
        ],
        scratch_shapes=[
            pltpu.VMEM((128, cols), F32),
            pltpu.VMEM((block, 128), F32),
            pltpu.VMEM((128, 128), F32),
            pltpu.VMEM(wmat.shape, wmat.dtype),
            pltpu.SMEM((block + 1,), I32),
            pltpu.SemaphoreType.DMA,
            pltpu.SemaphoreType.DMA,
        ],
        compiler_params=pltpu.CompilerParams(vmem_limit_bytes=67043328),
        name="pick",
    )(removed, removed, hess, wmat)


def group_of(index, size):
    return sum((index >= w * size).astype(I32) for w in range(1, 8))


def middle_kernel(index, parts, out, slot, *, size):
    block = index.shape[1]
    group = group_of(index[...], size).astype(F32)
    turned = jnp.broadcast_to(group, (8, block)).T[:, :1]
    first = lax.broadcasted_iota(I32, (block, block), 0)
    second = lax.broadcasted_iota(I32, (block, block), 1)
    same = turned == group
    before = jnp.sum((same & (first < second)).astype(F32), axis=0, keepdims=True)
    lane = (group * 128.0 + before).astype(I32)
    ahead = jnp.sum((same & (second < first)).astype(F32), axis=1, keepdims=True)
    slot[...] = (turned * float(ROOM) + ahead).astype(I32)
    lanes = []
    for w in range(8):
        total = parts[w * 16]
        for n in range(1, 16):
            total = total + parts[w * 16 + n]
        lanes.append(total)
    packed = jnp.concatenate(lanes, axis=1)
    rows = exact_dot(packed, hot_rows(8 * 128, lane))
    for d in range(128):
        out[d] = rows


def middle(index, parts, size):
    block = index.shape[1]
    return pl.pallas_call(
        functools.partial(middle_kernel, size=size),
        in_specs=[pl.BlockSpec(memory_space=VMEM)] * 2,
        out_specs=[pl.BlockSpec(memory_space=VMEM)] * 2,
        out_shape=[
            jax.ShapeDtypeStruct((128, block // 128, block), F32),
            jax.ShapeDtypeStruct((block, 1), I32),
        ],
        compiler_params=limit(16),
        name="middle",
    )(index, parts)


def inverse_kernel(tiles, out, full):
    block = full.shape[0]
    each = block // 128
    for d in range(128):
        full[d * each : (d + 1) * each, :] = tiles[d]
    a = full[...]
    total = jnp.sum(jnp.abs(a), axis=0, keepdims=True)
    scale = 1.0 / jnp.max(total)
    shape = (block, block)
    eye = (lax.broadcasted_iota(I32, shape, 0) == lax.broadcasted_iota(I32, shape, 1)).astype(F32)
    e = eye - a * scale
    p = (eye + e) * scale
    es = split(e)
    e = times(es, es)
    for turn in range(1, ITERS):
        es = split(e)
        if turn < ITERS - 1:
            e = times(es, es)
        p = p + times(split(p), es)
    out[...] = p


def inverse_of(tiles):
    block = tiles.shape[2]
    return pl.pallas_call(
        inverse_kernel,
        in_specs=[pl.BlockSpec(memory_space=VMEM)],
        out_specs=pl.BlockSpec(memory_space=VMEM),
        out_shape=jax.ShapeDtypeStruct((block, block), F32),
        scratch_shapes=[pltpu.VMEM((block, block), F32)],
        compiler_params=limit(16),
        cost_estimate=cost(14 * 3 * 2 * block**3, 8 * block**2),
        name="inverse",
    )(tiles)


def arrange_kernel(tab, slot, s0, s1, s2, s3, s4, s5, out, stack):
    at = lambda i: pl.ds(pl.multiple_of(tab[i] * ROOM, 16), ROOM)
    for i, part in enumerate((s0[...], s1[...], s2[0], s2[1], s3[0], s3[1], s4[...], s5[...])):
        stack[at(i), :] = part
    ids = lax.broadcasted_iota(I32, (slot.shape[0], 8 * ROOM), 1)
    hot = (ids == slot[...]).astype(BF16)
    cols = out.shape[1]
    for c in range(0, cols, 256):
        d = min(c + 256, cols)
        out[:, c:d] = dot(hot, stack[:, c:d]).astype(BF16)


def arrange(table, slot, groups):
    block = slot.shape[0]
    cols = groups[0].shape[-1]
    return pl.pallas_call(
        arrange_kernel,
        in_specs=[pl.BlockSpec(memory_space=SMEM)] + [pl.BlockSpec(memory_space=VMEM)] * 7,
        out_specs=pl.BlockSpec(memory_space=VMEM),
        out_shape=jax.ShapeDtypeStruct((block, cols), BF16),
        scratch_shapes=[pltpu.VMEM((8 * ROOM, cols), BF16)],
        compiler_params=limit(16),
        cost_estimate=cost(2 * block * 8 * ROOM * cols, 4 * block * cols),
    )(table, slot, *groups)


def finish_kernel(tab, index, inv, rows, mine, other, hess, wmat, hess_out, wmat_out,
                  held, both, wheld, wnew, sem_in, sem_out, sem_w):
    block = inv.shape[0]
    size, cols = hess.shape
    step = size // 8
    at = lambda t: pl.ds(pl.multiple_of(tab[t] * step, step), step)
    wcopy = pltpu.make_async_copy(wmat, wheld, sem_w.at[0])
    wcopy.start()
    loads = [pltpu.make_async_copy(hess.at[at(t), :], held.at[t], sem_in.at[t]) for t in range(8)]
    for load in loads:
        load.start()
    x_hi, x_lo = split(inv[...])
    for c in range(0, cols, 256):
        r = rows[:, c : c + 256]
        both[:, c : c + 256] = (dot(x_hi, r) + dot(x_lo, r)).astype(BF16)
    chosen = rows[:, cols:].T
    gain = (dot(chosen, x_hi) + dot(chosen, x_lo)).astype(BF16)
    picked = jnp.broadcast_to(index[...].astype(F32), (8, block)).T[:, :1].astype(I32)
    row_start = lax.axis_index("wide") * size
    wcopy.wait()
    stores = []
    for t in range(8):
        left = mine if t < 4 else other
        panel = left[:, (t % 4) * step : (t % 4 + 1) * step]
        turned = panel.T
        loads[t].wait()
        for c in range(0, cols, 512):
            held[t, :, c : c + 512] = held[t, :, c : c + 512] - dot(turned, both[:, c : c + 512])
        store = pltpu.make_async_copy(held.at[t], hess_out.at[at(t), :], sem_out.at[t])
        store.start()
        stores.append(store)
        ids = lax.broadcasted_iota(I32, (1, step), 1) + (row_start + tab[t] * step)
        hit = jnp.max((picked == ids).astype(F32), axis=0, keepdims=True)
        new = wheld[:, at(t)].astype(F32) - dot(gain, panel)
        wnew[:, at(t)] = jnp.where(hit > 0, 0.0, new).astype(BF16)
    last = pltpu.make_async_copy(wnew, wmat_out, sem_w.at[1])
    last.start()
    for store in stores:
        store.wait()
    last.wait()


def finish(order, index, inv, rows, mine, other, hess, wmat):
    block = inv.shape[0]
    size, cols = hess.shape
    vmem = pl.BlockSpec(memory_space=VMEM)
    anywhere = pl.BlockSpec(memory_space=pl.ANY)
    return pl.pallas_call(
        finish_kernel,
        in_specs=[pl.BlockSpec(memory_space=SMEM)] + [vmem] * 5 + [anywhere] * 2,
        out_specs=[anywhere] * 2,
        out_shape=[jax.ShapeDtypeStruct(hess.shape, F32), jax.ShapeDtypeStruct(wmat.shape, BF16)],
        scratch_shapes=[
            pltpu.VMEM((8, size // 8, cols), F32),
            pltpu.VMEM((block, cols), BF16),
            pltpu.VMEM(wmat.shape, BF16),
            pltpu.VMEM(wmat.shape, BF16),
            pltpu.SemaphoreType.DMA((8,)),
            pltpu.SemaphoreType.DMA((8,)),
            pltpu.SemaphoreType.DMA((2,)),
        ],
        compiler_params=limit(56),
        cost_estimate=cost(size * cols * block * 2, size * cols * 8),
        name="finish",
    )(order, index, inv, rows, mine, other, hess, wmat)


def ring_sum(a, axis):
    size = lax.axis_size(axis)

    def turn(k, carry):
        total, moving = carry
        moving = hop(moving, axis, size, lambda i: (i + 1) % size)
        return total + moving, moving

    return lax.fori_loop(0, size - 1, turn, (a, a))[0]


def masked_take(src, index, start, axis):
    size = src.shape[axis]
    shape = list(src.shape)
    shape[axis] = index.shape[0]

    def one(k, out):
        at = index[k] - start
        piece = lax.dynamic_slice_in_dim(src, jnp.clip(at, 0, size - 1), 1, axis)
        piece = jnp.where((at >= 0) & (at < size), piece.astype(F32), 0.0)
        return lax.dynamic_update_slice_in_dim(out, piece, k, axis)

    return lax.fori_loop(0, index.shape[0], one, jnp.zeros(shape, F32))


def general_gather(hess, wmat, removed, core):
    row_count, col_count = hess.shape
    row_start = lax.axis_index("wide") * row_count
    col_start = lax.axis_index("narrow") * col_count
    index = removed[0]
    block = index.shape[0]
    rows = ring_sum(masked_take(hess, index, row_start, 0), "wide")
    chosen = ring_sum(masked_take(wmat, index, row_start, 1), "wide")
    pivot = ring_sum(masked_take(rows, index, col_start, 1), "narrow")
    columns = ring_sum(masked_take(hess, index, col_start, 1), "narrow")
    half = row_count // 2
    mine = lax.dynamic_slice_in_dim(columns, core * half, half, 0).T.astype(BF16)
    panel = jnp.concatenate([rows, chosen.T], axis=1).astype(BF16)
    return pivot.reshape(128, block // 128, block), mine, panel


def packed_path(hess, wmat, removed):
    row_count, _ = hess.shape
    wide = lax.axis_index("wide")
    narrow = lax.axis_index("narrow")
    z_hi, y = wide // 4, wide % 4
    x, z_lo, core = narrow // 4, (narrow // 2) % 2, narrow % 2
    packed, plain, pivot = pick(hess, wmat, removed)

    parts = lax.all_to_all(pivot, BOTH, 0, 0)
    swap = []
    for w in range(8):
        for n in range(16):
            px, pz, pc = n // 4, (n // 2) % 2, n % 2
            tx, tz = (px + w // 2) % 4, pz ^ (w % 2)
            swap.append((w * 16 + n, (n // 2) * 16 + tx * 4 + tz * 2 + pc))
    col = lax.ppermute(plain, BOTH, swap)
    far = z_hi_swap(packed)
    spread, slot = middle(removed, parts, row_count)
    tiles = lax.all_to_all(spread, BOTH, 0, 0)

    mate = z_lo_swap(col)
    pair = jnp.stack([col, mate])
    ahead, behind = x_step(pair, 1), x_step(pair, -1)
    cols = [col, mate, ahead, behind, x_step(ahead[0], 1), x_step(behind[1], -1)]
    near = jnp.stack([packed, far])
    up, down = y_step(near, 1), y_step(near, -1)
    rows = [packed, far, up, down, y_step(up[0], 1), y_step(down[1], -1)]

    w_of, g_of = [], []
    for step in (0, -1, 1, 2):
        for flip in (0, 1):
            w_of.append(((z_hi + flip) % 2) * 4 + (y + step) % 4)
            g_of.append(((x + step - wide // 2) % 4) * 2 + (z_lo + flip + wide) % 2)
    mine = arrange(jnp.stack(g_of).astype(I32), slot, cols)
    panel = arrange(jnp.stack(w_of).astype(I32), slot, rows)
    group = group_of(removed, row_count)
    counts = jnp.sum((group == jnp.arange(8, dtype=I32)[:, None]).astype(I32), axis=1)
    crowded = jnp.max(counts) > ROOM

    def again(state):
        return (jnp.zeros((), bool),) + general_gather(hess, wmat, removed, core)

    _, tiles, mine, panel = lax.while_loop(lambda state: state[0], again, (crowded, tiles, mine, panel))
    other = core_swap(mine)
    inv = inverse_of(tiles)
    order = jnp.stack([(core ^ (t // 4)) * 4 + t % 4 for t in range(8)]).astype(I32)
    return finish(order, removed, inv, panel, mine, other, hess, wmat)


def solution(mesh):
    return jax.shard_map(
        packed_path,
        mesh=mesh,
        in_specs=(P("wide", "narrow"), P("narrow", "wide"), P()),
        out_specs=(P("wide", "narrow"), P("narrow", "wide")),
        check_vma=False,
    )
```
